32 devices in a mesh: req: 8 (over z, x), tp: 4 (over y, core).
Axes of the slice: x: 2, y: 2, z: 4, core: 2. Of those that a mesh axis runs over, the one named last changes fastest.
Arguments:
- hidden: bfloat16 [512, 2048], P('req')
- norm_gain: float32 [2048], replicated, may hold values from 0.5 to 1.5
- head_weight: bfloat16 [2048, 12288], P(None, ('req', 'tp'))
- targets: int32 [512], P('req'), may hold values from 0 to 12287
- pad_mask: int32 [512], P('req'), may hold values 0 or 1
Outputs:
- logprob: float32 [512], P('req')
- entropy: float32 [512], P('req')
The draws below stay inside these ranges and needn't reach their ends.
All inputs are finite; a program needn't handle non-finite values. No bound on the sum of `pad_mask` on one device may be relied on, other than what follows from the above.
Results may differ from the reference program's by a relative error of at most 0.0012.
Values may be sent and summed in bfloat16 or wider, within the bound.
A program may use at most 128 MiB of HBM per device.

```python
import math
import jax
import jax.numpy as jnp
import numpy as np
from jax import lax

D = 2048
VOC_DEV = 384
TOKENS = 512
VOCAB = 12288
N_TP = 4


def shared_parts(key):
    base_key = jax.random.fold_in(key, 11)
    base = jax.random.normal(base_key, (D, VOCAB), jnp.float32) * (3.0 * D ** (-0.5))
    unit = jax.random.normal(jax.random.fold_in(key, 14), (6, D), jnp.float32)
    chosen_cols = jax.random.randint(jax.random.fold_in(key, 12), (6,), 0, VOCAB - 1)
    chosen_rows = jax.random.randint(jax.random.fold_in(key, 13), (6,), 0, TOKENS)
    return (base, unit, chosen_cols, chosen_rows)


def draw_head_weight(key, part):
    base, unit, chosen_cols, chosen_rows = shared_parts(key)
    levels = [110.0, 150.0, 210.0, 110.0, 150.0, 210.0]
    for index in range(6):
        column = unit[index] * (levels[index] / D)
        base = base.at[:, chosen_cols[index]].set(column)
        base = base.at[:, chosen_cols[index] + 1].set(column * 0.99)
    return base.astype(jnp.bfloat16)


def draw_hidden(key, part):
    base, unit, chosen_cols, chosen_rows = shared_parts(key)
    values = jax.random.normal(jax.random.fold_in(key, 21), (TOKENS, D), jnp.float32)
    for index in range(6):
        values = values.at[chosen_rows[index], :].set(unit[index] * 2.0)
    return values.astype(jnp.bfloat16)


def set_ends(array, stream_key, low, largest):
    place = [jax.random.randint(jax.random.fold_in(stream_key, axis), (), 0, length) for axis, length in enumerate(array.shape)]
    main_axis = array.shape.index(max(array.shape))
    beside = place[:main_axis] + [(place[main_axis] + 1) % array.shape[main_axis]] + place[main_axis + 1:]
    return array.at[tuple(place)].set(low).at[tuple(beside)].set(largest)


def rank_bounds(amount, slope):
    loads = [(1 << 20) // math.isqrt(rank ** slope) + 1 for rank in range(1, amount + 1)]
    deviation = 1 + sum(loads) // (1 << 30)
    return np.cumsum(np.array([max(1, weight // deviation) for weight in loads]))


def ranked_ids(stream_key, shape, amount, skew):
    table = rank_bounds(amount, skew)
    pick = jax.random.randint(jax.random.fold_in(stream_key, 1), shape, 0, int(table[amount - 1]))
    standing = jnp.searchsorted(jnp.asarray(table, jnp.int32), pick, side="right")
    return jax.random.permutation(jax.random.fold_in(stream_key, 2), amount)[standing].astype(jnp.int32)


def setup_inputs(seed: int = 0) -> dict:
    splits = jax.random.split(jax.random.key(seed), 6)
    return {
        "hidden": draw_hidden(jax.random.fold_in(splits[5], 71), 0),
        "norm_gain": jnp.clip(1.0 + 0.1 * jax.random.normal(splits[1], (D,), jnp.float32), 0.5, 1.5),
        "head_weight": draw_head_weight(jax.random.fold_in(splits[5], 71), 0),
        "targets": set_ends(ranked_ids(splits[3], (TOKENS,), VOCAB, 2), jax.random.fold_in(splits[3], 3), 0, VOCAB - 1).astype(jnp.int32),
        "pad_mask": set_ends((jax.random.randint(splits[4], (TOKENS,), 0, 4) < 3).astype(jnp.int32), jax.random.fold_in(splits[4], 1), 0, 1),
    }


def combine_stats(earlier, later):
    top_a, total_a, weighted_a, picked_a = earlier
    top_b, total_b, weighted_b, picked_b = later
    top_new = jnp.maximum(top_a, top_b)
    scale_a = jnp.exp(top_a - top_new)
    scale_b = jnp.exp(top_b - top_new)
    return (top_new, total_a * scale_a + total_b * scale_b, weighted_a * scale_a + weighted_b * scale_b, picked_a + picked_b)

def reference(hidden, norm_gain, head_weight, targets, pad_mask):
    wide = hidden.astype(jnp.float32)
    scale = lax.rsqrt(lax.optimization_barrier(jnp.mean(wide * wide, axis=1, keepdims=True)) + 1e-05)
    normed = (wide * scale * norm_gain[None, :]).astype(jnp.bfloat16)
    block = VOC_DEV * N_TP
    count = head_weight.shape[1] // block
    blocks = head_weight.reshape(head_weight.shape[0], count, block).transpose(1, 0, 2)
    columns = lax.broadcasted_iota(jnp.int32, (1, block), 1)

    def step(carry, inputs):
        weight_block, index = inputs
        logits = jnp.dot(normed, weight_block, preferred_element_type=jnp.float32)
        top_row = lax.optimization_barrier(jnp.max(logits, axis=1))
        expo = jnp.exp(logits - top_row[:, None])
        local = targets.astype(jnp.int32) - index * block
        picked_row = lax.optimization_barrier(jnp.sum(jnp.where(columns == local[:, None], logits, jnp.float32(0.0)), axis=1))
        part = (top_row, lax.optimization_barrier(jnp.sum(expo, axis=1)), lax.optimization_barrier(jnp.sum(expo * logits, axis=1)), picked_row)
        return (combine_stats(carry, part), None)
    rows = hidden.shape[0]
    start = (jnp.full((rows,), -jnp.inf, jnp.float32), jnp.zeros((rows,), jnp.float32), jnp.zeros((rows,), jnp.float32), jnp.zeros((rows,), jnp.float32))
    indices = jnp.arange(count, dtype=jnp.int32)
    final, unused = lax.scan(step, start, (blocks, indices))
    top_all, total_all, weighted_all, picked_all = final
    lse = top_all + jnp.log(total_all)
    live = pad_mask.astype(jnp.float32)
    logprob = (picked_all - lse) * live
    entropy = (lse - weighted_all / total_all) * live
    return (logprob, entropy)
```

```python
import functools

import jax
import jax.numpy as jnp
from jax import lax
from jax.experimental import pallas as pl
from jax.experimental.pallas import tpu as pltpu
from jax.sharding import PartitionSpec as P

MESH = pl.DeviceIdType.MESH
EPS = 1e-05


def general_body(hidden, norm_gain, head_weight, targets, pad_mask):
    slots = hidden.shape[0]
    voc_local = head_weight.shape[1]
    tp_count = lax.axis_size("tp")
    voc_start = (lax.axis_index("req") * tp_count + lax.axis_index("tp")) * voc_local
    wide = hidden.astype(jnp.float32)
    scale = lax.rsqrt(jnp.mean(wide * wide, axis=1, keepdims=True) + EPS)
    normed = (wide * scale * norm_gain[None, :]).astype(jnp.bfloat16)
    columns = lax.broadcasted_iota(jnp.int32, (1, voc_local), 1)
    all_targets = lax.all_gather(targets, "req", axis=0, tiled=True)
    logits = jnp.dot(
        lax.all_gather(normed, "req", axis=0, tiled=True),
        head_weight,
        preferred_element_type=jnp.float32,
    )
    top = jnp.max(logits, axis=1)
    expo = jnp.exp(logits - top[:, None])
    local = all_targets - voc_start
    picked = jnp.sum(jnp.where(columns == local[:, None], logits, 0.0), axis=1)
    stats = jnp.stack([top, jnp.sum(expo, axis=1), jnp.sum(expo * logits, axis=1), picked])
    every = lax.all_gather(stats, ("req", "tp"))
    own = lax.axis_index("req") * slots
    every = lax.dynamic_slice_in_dim(every, own, slots, 2)
    top_all = jnp.max(every[:, 0], axis=0)
    share = jnp.exp(every[:, 0] - top_all[None])
    total = jnp.sum(every[:, 1] * share, axis=0)
    weighted = jnp.sum(every[:, 2] * share, axis=0)
    lse = top_all + jnp.log(total)
    live = pad_mask.astype(jnp.float32)
    logprob = (jnp.sum(every[:, 3], axis=0) - lse) * live
    entropy = (lse - weighted / total) * live
    return (logprob, entropy)


X, A1, A2, A3, B1, B2, B3 = range(7)
Y_OF = {A2: 7, A3: 8, B1: 9, B2: 10, B3: 11}
CORE_HALF = {X: 12, A1: 13}
CORE_NEAR = {A2: 14, A3: 15, B1: 16, B2: 17, B3: 18}
CORE_FAR = {A2: 19, A3: 20, B1: 21, B2: 22, B3: 23}
N_COPIES = 24


def kernel(
    hidden, gain, weight_hbm, targets, mask,
    logprob, entropy,
    rows, weight, tgt, outbox, inbox,
    w_sem, send, recv, tgt_send, tgt_recv, stat_send, stat_recv,
):
    slots, depth = hidden.shape
    voc = weight.shape[1]
    half, quarter = slots // 2, slots // 4
    req, tp = lax.axis_index("req"), lax.axis_index("tp")
    me = req * 4 + tp
    z, x = req // 2, req % 2
    y, c = tp // 2, tp % 2

    load = pltpu.make_async_copy(weight_hbm, weight, w_sem)
    load.start()

    barrier = pltpu.get_barrier_semaphore()
    for k in range(1, 32):
        other = (me + k) % 32
        pl.semaphore_signal(barrier, inc=1, device_id=(other // 4, other % 4), device_id_type=MESH)

    def norm_half(core):
        wide = hidden[pl.ds(pl.multiple_of(core * half, half), half), :].astype(jnp.float32)
        scale = lax.rsqrt(jnp.mean(wide * wide, axis=1, keepdims=True) + EPS)
        start = pl.multiple_of(req * slots + core * half, half)
        rows[pl.ds(start, half), :] = (wide * scale * gain[...]).astype(jnp.bfloat16)

    norm_half(c)
    tgt[req] = jnp.concatenate([targets[...], jnp.zeros((1, 128 - slots), jnp.int32)], axis=1)
    pl.semaphore_wait(barrier, 31)

    z1 = z + 1 - 2 * (z % 2)
    z2 = (z + 2) % 4
    z3 = 3 - z
    xo = 1 - x
    block = {X: z * 2 + xo, A1: z1 * 2 + x, A2: z2 * 2 + x, A3: z3 * 2 + x,
             B1: z1 * 2 + xo, B2: z2 * 2 + xo, B3: z3 * 2 + xo}
    x_dev, y_dev, core_dev = (z * 2 + xo, tp), (req, (1 - y) * 2 + c), (req, y * 2 + 1 - c)

    def half_rows(b, core):
        return rows.at[pl.ds(pl.multiple_of(b * slots + core * half, half), half), :]

    def quarter_rows(b, core, side):
        start = b * slots + core * half + side * quarter
        return rows.at[pl.ds(pl.multiple_of(start, quarter), quarter), :]

    started = []

    def push(piece, index, device):
        copy = pltpu.make_async_remote_copy(
            src_ref=piece, dst_ref=piece, send_sem=send.at[index], recv_sem=recv.at[index],
            device_id=device, device_id_type=MESH,
        )
        copy.start()
        started.append(copy)

    def arrived(piece, index):
        pltpu.make_async_copy(piece, piece, recv.at[index]).wait()

    push(quarter_rows(req, c, y), A3, (block[A3], tp))
    push(half_rows(req, c), X, x_dev)
    push(quarter_rows(req, c, y), A2, (block[A2], tp))
    push(half_rows(req, c), A1, (block[A1], tp))
    tgt_copies = []
    for k in range(1, 8):
        other = (req + k) % 8
        copy = pltpu.make_async_remote_copy(
            src_ref=tgt.at[req], dst_ref=tgt.at[req], send_sem=tgt_send.at[k - 1],
            recv_sem=tgt_recv.at[k - 1], device_id=(other, tp), device_id_type=MESH,
        )
        copy.start()
        tgt_copies.append(copy)
    norm_half(1 - c)

    eye = lax.broadcasted_iota(jnp.int32, (slots, slots), 0) == lax.broadcasted_iota(
        jnp.int32, (slots, slots), 1)
    eye2 = lax.broadcasted_iota(jnp.int32, (2 * slots, 2 * slots), 0) == lax.broadcasted_iota(
        jnp.int32, (2 * slots, 2 * slots), 1)
    voc_ids = lax.broadcasted_iota(jnp.int32, (2 * slots, voc), 1) + me * voc

    def compute(index, plane):
        lhs = rows[pl.ds(pl.multiple_of(plane * 2 * slots, 2 * slots), 2 * slots), :]
        logits = jnp.dot(lhs, weight[...], preferred_element_type=jnp.float32)
        wanted = jnp.concatenate([
            jnp.sum(jnp.where(eye, tgt[plane * 2 + i][:, :slots], 0), axis=1, keepdims=True)
            for i in range(2)
        ], axis=0)
        top = jnp.max(logits, axis=1, keepdims=True)
        expo = jnp.exp(logits - top)
        parts = (
            top,
            jnp.sum(expo, axis=1, keepdims=True),
            jnp.sum(expo * logits, axis=1, keepdims=True),
            jnp.sum(jnp.where(voc_ids == wanted, logits, 0.0), axis=1, keepdims=True),
        )
        outbox[index] = jnp.concatenate(
            [jnp.sum(jnp.where(eye2, part, 0.0), axis=0, keepdims=True) for part in parts], axis=0)
        for k in range(8):
            if index == 0:
                if k == 0:
                    inbox[me] = outbox[index]
                    continue
                other = z * 8 + (me + k) % 8
            else:
                other = plane * 8 + (me + k) % 8
            pltpu.make_async_remote_copy(
                src_ref=outbox.at[index], dst_ref=inbox.at[me], send_sem=stat_send,
                recv_sem=stat_recv, device_id=(other // 4, other % 4), device_id_type=MESH,
            ).start()

    def near(kind):
        piece = quarter_rows(block[kind], c, y)
        arrived(piece, kind)
        if kind in (A2, A3):
            push(piece, kind - A1 + B1, x_dev)
        push(piece, Y_OF[kind], y_dev)
        push(piece, CORE_NEAR[kind], core_dev)

    def far(kind):
        piece = quarter_rows(block[kind], c, 1 - y)
        arrived(piece, Y_OF[kind])
        push(piece, CORE_FAR[kind], core_dev)

    def from_core(kind):
        if kind in CORE_HALF:
            arrived(half_rows(block[kind], 1 - c), CORE_HALF[kind])
        else:
            arrived(quarter_rows(block[kind], 1 - c, y), CORE_NEAR[kind])
            arrived(quarter_rows(block[kind], 1 - c, 1 - y), CORE_FAR[kind])

    arrived(half_rows(block[A1], c), A1)
    push(quarter_rows(block[A1], c, y), B1, x_dev)
    push(half_rows(block[A1], c), CORE_HALF[A1], core_dev)
    arrived(half_rows(block[X], c), X)
    push(half_rows(block[X], c), CORE_HALF[X], core_dev)
    near(A2)
    near(A3)
    load.wait()
    for copy in tgt_copies:
        copy.wait()
    from_core(X)
    compute(0, z)
    near(B1)
    near(B2)
    near(B3)
    far(A2)
    far(A3)
    far(B1)
    from_core(A1)
    from_core(B1)
    compute(1, z1)
    far(B2)
    far(B3)
    from_core(A2)
    from_core(B2)
    compute(2, z2)
    from_core(A3)
    from_core(B3)
    compute(3, z3)

    most = inbox.at[pl.ds(0, 31)]
    pltpu.make_async_copy(most, most, stat_recv).wait()
    every = inbox[...]
    tops = every[:, 0:1, :]
    top = jnp.max(tops, axis=0)
    share = jnp.exp(tops - top[None])
    total = jnp.sum(every[:, 1:2, :] * share, axis=0)
    weighted = jnp.sum(every[:, 2:3, :] * share, axis=0)
    picked = jnp.sum(every[:, 3:4, :], axis=0)
    lse = top + jnp.log(total)
    live = mask[...].astype(jnp.float32)
    own = lambda row: jnp.where(x == 0, row[:, :slots], row[:, slots:])
    logprob[...] = own(picked - lse) * live
    entropy[...] = own(lse - weighted / total) * live

    for copy in started:
        copy.wait_send()
    pltpu.make_async_copy(most, most, stat_send).wait()


def fused_body(hidden, norm_gain, head_weight, targets, pad_mask):
    slots, depth = hidden.shape
    voc = head_weight.shape[1]
    vmem = pl.BlockSpec(memory_space=pltpu.VMEM)
    row = jax.ShapeDtypeStruct((1, slots), jnp.float32)
    logprob, entropy = pl.pallas_call(
        kernel,
        out_shape=(row, row),
        in_specs=[vmem, vmem, pl.BlockSpec(memory_space=pl.ANY), vmem, vmem],
        out_specs=(vmem, vmem),
        scratch_shapes=[
            pltpu.VMEM((8 * slots, depth), jnp.bfloat16),
            pltpu.VMEM((depth, voc), jnp.bfloat16),
            pltpu.VMEM((8, 1, 128), jnp.int32),
            pltpu.VMEM((4, 4, 128), jnp.float32),
            pltpu.VMEM((32, 4, 128), jnp.float32),
            pltpu.SemaphoreType.DMA,
            pltpu.SemaphoreType.DMA((N_COPIES,)),
            pltpu.SemaphoreType.DMA((N_COPIES,)),
            pltpu.SemaphoreType.DMA((7,)),
            pltpu.SemaphoreType.DMA((7,)),
            pltpu.SemaphoreType.DMA,
            pltpu.SemaphoreType.DMA,
        ],
        compiler_params=pltpu.CompilerParams(
            collective_id=0, has_side_effects=True, vmem_limit_bytes=32 * 1024 * 1024),
    )(hidden, norm_gain.reshape(1, depth), head_weight, targets.reshape(1, slots),
      pad_mask.reshape(1, slots))
    return (logprob.reshape(slots), entropy.reshape(slots))


def solution(mesh):
    fused = mesh.shape["req"] == 8 and mesh.shape["tp"] == 4
    return jax.shard_map(
        fused_body if fused else general_body,
        mesh=mesh,
        in_specs=(P("req", None), P(), P(None, ("req", "tp")), P("req"), P("req")),
        out_specs=(P("req"), P("req")),
        check_vma=False,
    )
```

```python
import functools

import jax
import jax.numpy as jnp
from jax import lax
from jax.experimental import pallas as pl
from jax.experimental.pallas import tpu as pltpu
from jax.sharding import PartitionSpec as P

MESH = pl.DeviceIdType.MESH
EPS = 1e-05


def general_body(hidden, norm_gain, head_weight, targets, pad_mask):
    slots = hidden.shape[0]
    voc_local = head_weight.shape[1]
    tp_count = lax.axis_size("tp")
    voc_start = (lax.axis_index("req") * tp_count + lax.axis_index("tp")) * voc_local
    wide = hidden.astype(jnp.float32)
    scale = lax.rsqrt(jnp.mean(wide * wide, axis=1, keepdims=True) + EPS)
    normed = (wide * scale * norm_gain[None, :]).astype(jnp.bfloat16)
    columns = lax.broadcasted_iota(jnp.int32, (1, voc_local), 1)
    all_targets = lax.all_gather(targets, "req", axis=0, tiled=True)
    logits = jnp.dot(
        lax.all_gather(normed, "req", axis=0, tiled=True),
        head_weight,
        preferred_element_type=jnp.float32,
    )
    top = jnp.max(logits, axis=1)
    expo = jnp.exp(logits - top[:, None])
    local = all_targets - voc_start
    picked = jnp.sum(jnp.where(columns == local[:, None], logits, 0.0), axis=1)
    stats = jnp.stack([top, jnp.sum(expo, axis=1), jnp.sum(expo * logits, axis=1), picked])
    every = lax.all_gather(stats, ("req", "tp"))
    own = lax.axis_index("req") * slots
    every = lax.dynamic_slice_in_dim(every, own, slots, 2)
    top_all = jnp.max(every[:, 0], axis=0)
    share = jnp.exp(every[:, 0] - top_all[None])
    total = jnp.sum(every[:, 1] * share, axis=0)
    weighted = jnp.sum(every[:, 2] * share, axis=0)
    lse = top_all + jnp.log(total)
    live = pad_mask.astype(jnp.float32)
    logprob = (jnp.sum(every[:, 3], axis=0) - lse) * live
    entropy = (lse - weighted / total) * live
    return (logprob, entropy)


X, A1, A2, A3, B1, B2, B3, XP, A1P, A2P, A3P, B1P, B2P, B3P = range(14)
OTHER_Y = {X: XP, A1: A1P, A2: A2P, A3: A3P, B1: B1P, B2: B2P, B3: B3P}
CORE = 14
N_COPIES = 28
SUBS = 1


def kernel(
    hidden_hbm, gain_hbm, weight_hbm, targets_hbm,
    result,
    hidden, gain, targets, rows, weight, tgt, outbox, inbox,
    in_sems, w_sem, send, recv, tgt_send, tgt_recv, stat_send, stat_recv,
):
    slots, depth = hidden.shape
    voc = weight.shape[1]
    half, quarter = slots // 2, slots // 4
    req, tp = lax.axis_index("req"), lax.axis_index("tp")
    me = req * 4 + tp
    z, x = req // 2, req % 2
    y, c = tp // 2, tp % 2

    small = [
        pltpu.make_async_copy(hidden_hbm, hidden, in_sems.at[0]),
        pltpu.make_async_copy(gain_hbm, gain, in_sems.at[1]),
        pltpu.make_async_copy(targets_hbm, targets, in_sems.at[2]),
    ]
    for copy in small:
        copy.start()
    load = pltpu.make_async_copy(weight_hbm, weight, w_sem)
    load.start()

    barrier = pltpu.get_barrier_semaphore()
    for k in range(1, 32):
        other = (me + k) % 32
        pl.semaphore_signal(barrier, inc=1, device_id=(other // 4, other % 4), device_id_type=MESH)

    def norm_half(core):
        wide = hidden[pl.ds(pl.multiple_of(core * half, half), half), :].astype(jnp.float32)
        scale = lax.rsqrt(jnp.mean(wide * wide, axis=1, keepdims=True) + EPS)
        start = pl.multiple_of(req * slots + core * half, half)
        rows[pl.ds(start, half), :] = (wide * scale * gain[...]).astype(jnp.bfloat16)

    for copy in small:
        copy.wait()
    norm_half(c)
    tgt[req] = jnp.concatenate([targets[...], jnp.zeros((1, 128 - slots), jnp.int32)], axis=1)
    pl.semaphore_wait(barrier, 31)

    z1 = z + 1 - 2 * (z % 2)
    z2 = (z + 2) % 4
    z3 = 3 - z
    xo = 1 - x
    block = {X: z * 2 + xo, A1: z1 * 2 + x, A2: z2 * 2 + x, A3: z3 * 2 + x,
             B1: z1 * 2 + xo, B2: z2 * 2 + xo, B3: z3 * 2 + xo}
    x_dev, y_dev, core_dev = (z * 2 + xo, tp), (req, (1 - y) * 2 + c), (req, y * 2 + 1 - c)
    diag_dev = (z * 2 + xo, (1 - y) * 2 + c)

    for kind in OTHER_Y:
        block[OTHER_Y[kind]] = block[kind]

    def piece_of(b, core, side, sub):
        start = pl.multiple_of(b * slots + core * half + side * quarter, quarter)
        width = depth // SUBS
        return rows.at[pl.ds(start, quarter), pl.ds(sub * width, width)]

    started = []

    def push(piece, kind, sub, device):
        index = kind * SUBS + sub
        copy = pltpu.make_async_remote_copy(
            src_ref=piece, dst_ref=piece, send_sem=send.at[index], recv_sem=recv.at[index],
            device_id=device, device_id_type=MESH,
        )
        copy.start()
        started.append(copy)

    def arrived(piece, kind, sub):
        pltpu.make_async_copy(piece, piece, recv.at[kind * SUBS + sub]).wait()

    z_dev = {A1: (block[A1], tp), A2: (block[A2], tp), A3: (block[A3], tp), X: x_dev}

    def give(kind):
        target, side = (kind, y) if kind < XP else (kind - XP, 1 - y)
        for sub in range(SUBS):
            push(piece_of(req, c, side, sub), kind, sub, z_dev[target])

    give(A3)
    give(X)
    give(A1)
    tgt_copies = []
    for k in range(1, 8):
        other = (req + k) % 8
        copy = pltpu.make_async_remote_copy(
            src_ref=tgt.at[req], dst_ref=tgt.at[req], send_sem=tgt_send.at[k - 1],
            recv_sem=tgt_recv.at[k - 1], device_id=(other, tp), device_id_type=MESH,
        )
        copy.start()
        tgt_copies.append(copy)
    norm_half(1 - c)
    started.pop(0).wait_send()
    give(A2)

    eye = lax.broadcasted_iota(jnp.int32, (slots, slots), 0) == lax.broadcasted_iota(
        jnp.int32, (slots, slots), 1)
    eye2 = lax.broadcasted_iota(jnp.int32, (2 * slots, 2 * slots), 0) == lax.broadcasted_iota(
        jnp.int32, (2 * slots, 2 * slots), 1)
    voc_ids = lax.broadcasted_iota(jnp.int32, (2 * slots, voc), 1) + me * voc

    def compute(index, plane):
        lhs = rows[pl.ds(pl.multiple_of(plane * 2 * slots, 2 * slots), 2 * slots), :]
        logits = jnp.dot(lhs, weight[...], preferred_element_type=jnp.float32)
        wanted = jnp.concatenate([
            jnp.sum(jnp.where(eye, tgt[plane * 2 + i][:, :slots], 0), axis=1, keepdims=True)
            for i in range(2)
        ], axis=0)
        top = jnp.max(logits, axis=1, keepdims=True)
        expo = jnp.exp(logits - top)
        parts = (
            top,
            jnp.sum(expo, axis=1, keepdims=True),
            jnp.sum(expo * logits, axis=1, keepdims=True),
            jnp.sum(jnp.where(voc_ids == wanted, logits, 0.0), axis=1, keepdims=True),
        )
        outbox[index] = jnp.concatenate(
            [jnp.sum(jnp.where(eye2, part, 0.0), axis=0, keepdims=True) for part in parts], axis=0)
        for k in range(8):
            if plane is z:
                if k == 0:
                    inbox[me] = outbox[index]
                    continue
                other = z * 8 + (me + k) % 8
            else:
                other = plane * 8 + (me + k) % 8
            pltpu.make_async_remote_copy(
                src_ref=outbox.at[index], dst_ref=inbox.at[me], send_sem=stat_send,
                recv_sem=stat_recv, device_id=(other // 4, other % 4), device_id_type=MESH,
            ).start()

    routes = {A1: [(B1, x_dev)], A2: [(B2, x_dev), (A2P, y_dev)], A3: [(B3, x_dev), (A3P, y_dev)], B1: [(B1P, y_dev)], B2: [(B2P, y_dev)], B3: [(B3P, y_dev)]}

    def take(*kinds):
        for kind in kinds:
            for sub in range(SUBS):
                piece = piece_of(block[kind], c, y if kind < XP else 1 - y, sub)
                arrived(piece, kind, sub)
                for later, device in routes.get(kind, ()):
                    push(piece, later, sub, device)
                push(piece, CORE + kind, sub, core_dev)

    def from_core(*kinds):
        for kind in kinds:
            for side, k in ((y, kind), (1 - y, OTHER_Y[kind])):
                for sub in range(SUBS):
                    arrived(piece_of(block[kind], 1 - c, side, sub), CORE + k, sub)

    take(A3)
    give(A1P)
    take(X, A2, A1)
    give(XP)
    take(B3, A3P, B2, A2P, B1)
    load.wait()
    for copy in tgt_copies:
        copy.wait()
    take(B3P)
    from_core(A3, B3)
    compute(0, z3)
    take(XP, A1P, B2P)
    from_core(A2, B2)
    compute(1, z2)
    take(B1P)
    from_core(X)
    compute(2, z)
    from_core(A1, B1)
    compute(3, z1)

    most = inbox.at[pl.ds(0, 31)]
    pltpu.make_async_copy(most, most, stat_recv).wait()
    every = inbox[...]
    tops = every[:, 0:1, :]
    top = jnp.max(tops, axis=0)
    share = jnp.exp(tops - top[None])
    total = jnp.sum(every[:, 1:2, :] * share, axis=0)
    weighted = jnp.sum(every[:, 2:3, :] * share, axis=0)
    picked = jnp.sum(every[:, 3:4, :], axis=0)
    lse = top + jnp.log(total)
    both = jnp.concatenate([picked - lse, lse - weighted / total], axis=0)
    result[...] = jnp.where(x == 0, both[:, :slots], both[:, slots:])

    for copy in started:
        copy.wait_send()
    pltpu.make_async_copy(most, most, stat_send).wait()


def fused_body(hidden, norm_gain, head_weight, targets, pad_mask):
    slots, depth = hidden.shape
    voc = head_weight.shape[1]
    vmem = pl.BlockSpec(memory_space=pltpu.VMEM)
    hbm = pl.BlockSpec(memory_space=pltpu.HBM)
    result = pl.pallas_call(
        kernel,
        out_shape=jax.ShapeDtypeStruct((2, slots), jnp.float32),
        in_specs=[hbm] * 4,
        out_specs=vmem,
        scratch_shapes=[
            pltpu.VMEM((slots, depth), jnp.bfloat16),
            pltpu.VMEM((1, depth), jnp.float32),
            pltpu.VMEM((1, slots), jnp.int32),
            pltpu.VMEM((8 * slots, depth), jnp.bfloat16),
            pltpu.VMEM((depth, voc), jnp.bfloat16),
            pltpu.VMEM((8, 1, 128), jnp.int32),
            pltpu.VMEM((4, 4, 128), jnp.float32),
            pltpu.VMEM((32, 4, 128), jnp.float32),
            pltpu.SemaphoreType.DMA((3,)),
            pltpu.SemaphoreType.DMA,
            pltpu.SemaphoreType.DMA((N_COPIES * SUBS,)),
            pltpu.SemaphoreType.DMA((N_COPIES * SUBS,)),
            pltpu.SemaphoreType.DMA((7,)),
            pltpu.SemaphoreType.DMA((7,)),
            pltpu.SemaphoreType.DMA,
            pltpu.SemaphoreType.DMA,
        ],
        compiler_params=pltpu.CompilerParams(
            collective_id=0, has_side_effects=True, vmem_limit_bytes=60 * 1024 * 1024),
    )(hidden, norm_gain.reshape(1, depth), head_weight, targets.reshape(1, slots))
    live = pad_mask.astype(jnp.float32)
    return (result[0] * live, result[1] * live)


def solution(mesh):
    fused = mesh.shape["req"] == 8 and mesh.shape["tp"] == 4
    return jax.shard_map(
        fused_body if fused else general_body,
        mesh=mesh,
        in_specs=(P("req", None), P(), P(None, ("req", "tp")), P("req"), P("req")),
        out_specs=(P("req"), P("req")),
        check_vma=False,
    )
```

```python
import functools

import jax
import jax.numpy as jnp
from jax import lax
from jax.experimental import pallas as pl
from jax.experimental.pallas import tpu as pltpu
from jax.sharding import PartitionSpec as P

MESH = pl.DeviceIdType.MESH
EPS = 1e-05


def general_body(hidden, norm_gain, head_weight, targets, pad_mask):
    slots = hidden.shape[0]
    voc_local = head_weight.shape[1]
    tp_count = lax.axis_size("tp")
    voc_start = (lax.axis_index("req") * tp_count + lax.axis_index("tp")) * voc_local
    wide = hidden.astype(jnp.float32)
    scale = lax.rsqrt(jnp.mean(wide * wide, axis=1, keepdims=True) + EPS)
    normed = (wide * scale * norm_gain[None, :]).astype(jnp.bfloat16)
    columns = lax.broadcasted_iota(jnp.int32, (1, voc_local), 1)
    all_targets = lax.all_gather(targets, "req", axis=0, tiled=True)
    logits = jnp.dot(
        lax.all_gather(normed, "req", axis=0, tiled=True),
        head_weight,
        preferred_element_type=jnp.float32,
    )
    top = jnp.max(logits, axis=1)
    expo = jnp.exp(logits - top[:, None])
    local = all_targets - voc_start
    picked = jnp.sum(jnp.where(columns == local[:, None], logits, 0.0), axis=1)
    stats = jnp.stack([top, jnp.sum(expo, axis=1), jnp.sum(expo * logits, axis=1), picked])
    every = lax.all_gather(stats, ("req", "tp"))
    own = lax.axis_index("req") * slots
    every = lax.dynamic_slice_in_dim(every, own, slots, 2)
    top_all = jnp.max(every[:, 0], axis=0)
    share = jnp.exp(every[:, 0] - top_all[None])
    total = jnp.sum(every[:, 1] * share, axis=0)
    weighted = jnp.sum(every[:, 2] * share, axis=0)
    lse = top_all + jnp.log(total)
    live = pad_mask.astype(jnp.float32)
    logprob = (jnp.sum(every[:, 3], axis=0) - lse) * live
    entropy = (lse - weighted / total) * live
    return (logprob, entropy)


X, A1, A2, A3, B1, B2, B3, XP, A1P, A2P, A3P, B1P, B2P, B3P = range(14)
OTHER_Y = {X: XP, A1: A1P, A2: A2P, A3: A3P, B1: B1P, B2: B2P, B3: B3P}
CORE = 14
N_COPIES = 28
SUBS = 2


def kernel(
    hidden_hbm, gain_hbm, weight_hbm, targets_hbm,
    result,
    hidden, gain, targets, rows, weight, tgt, outbox, inbox,
    in_sems, w_sem, send, recv, tgt_send, tgt_recv, stat_send, stat_recv,
):
    slots, depth = hidden.shape
    voc = weight.shape[1]
    half, quarter = slots // 2, slots // 4
    req, tp = lax.axis_index("req"), lax.axis_index("tp")
    me = req * 4 + tp
    z, x = req // 2, req % 2
    y, c = tp // 2, tp % 2

    small = [
        pltpu.make_async_copy(hidden_hbm, hidden, in_sems.at[0]),
        pltpu.make_async_copy(gain_hbm, gain, in_sems.at[1]),
        pltpu.make_async_copy(targets_hbm, targets, in_sems.at[2]),
    ]
    for copy in small:
        copy.start()
    load = pltpu.make_async_copy(weight_hbm, weight, w_sem)
    load.start()

    barrier = pltpu.get_barrier_semaphore()
    for k in range(1, 32):
        other = (me + k) % 32
        pl.semaphore_signal(barrier, inc=1, device_id=(other // 4, other % 4), device_id_type=MESH)

    def norm_half(core):
        wide = hidden[pl.ds(pl.multiple_of(core * half, half), half), :].astype(jnp.float32)
        scale = lax.rsqrt(jnp.mean(wide * wide, axis=1, keepdims=True) + EPS)
        start = pl.multiple_of(req * slots + core * half, half)
        rows[pl.ds(start, half), :] = (wide * scale * gain[...]).astype(jnp.bfloat16)

    for copy in small:
        copy.wait()
    norm_half(c)
    tgt[req] = jnp.concatenate([targets[...], jnp.zeros((1, 128 - slots), jnp.int32)], axis=1)
    pl.semaphore_wait(barrier, 31)

    z1 = z + 1 - 2 * (z % 2)
    z2 = (z + 2) % 4
    z3 = 3 - z
    xo = 1 - x
    block = {X: z * 2 + xo, A1: z1 * 2 + x, A2: z2 * 2 + x, A3: z3 * 2 + x,
             B1: z1 * 2 + xo, B2: z2 * 2 + xo, B3: z3 * 2 + xo}
    x_dev, y_dev, core_dev = (z * 2 + xo, tp), (req, (1 - y) * 2 + c), (req, y * 2 + 1 - c)
    diag_dev = (z * 2 + xo, (1 - y) * 2 + c)

    for kind in OTHER_Y:
        block[OTHER_Y[kind]] = block[kind]

    def piece_of(b, core, side, sub):
        start = pl.multiple_of(b * slots + core * half + side * quarter, quarter)
        width = depth // SUBS
        return rows.at[pl.ds(start, quarter), pl.ds(sub * width, width)]

    started = []

    def push(piece, kind, sub, device):
        index = kind * SUBS + sub
        copy = pltpu.make_async_remote_copy(
            src_ref=piece, dst_ref=piece, send_sem=send.at[index], recv_sem=recv.at[index],
            device_id=device, device_id_type=MESH,
        )
        copy.start()
        started.append(copy)

    def arrived(piece, kind, sub):
        pltpu.make_async_copy(piece, piece, recv.at[kind * SUBS + sub]).wait()

    z_dev = {A1: (block[A1], tp), A2: (block[A2], tp), A3: (block[A3], tp), X: x_dev}

    def give(kind):
        target, side = (kind, y) if kind < XP else (kind - XP, 1 - y)
        for sub in range(SUBS):
            push(piece_of(req, c, side, sub), kind, sub, z_dev[target])

    give(A3)
    give(X)
    give(A1)
    tgt_copies = []
    for k in range(1, 8):
        other = (req + k) % 8
        copy = pltpu.make_async_remote_copy(
            src_ref=tgt.at[req], dst_ref=tgt.at[req], send_sem=tgt_send.at[k - 1],
            recv_sem=tgt_recv.at[k - 1], device_id=(other, tp), device_id_type=MESH,
        )
        copy.start()
        tgt_copies.append(copy)
    norm_half(1 - c)
    started.pop(0).wait_send()
    give(A2)

    eye = lax.broadcasted_iota(jnp.int32, (slots, slots), 0) == lax.broadcasted_iota(
        jnp.int32, (slots, slots), 1)
    eye2 = lax.broadcasted_iota(jnp.int32, (2 * slots, 2 * slots), 0) == lax.broadcasted_iota(
        jnp.int32, (2 * slots, 2 * slots), 1)
    voc_ids = lax.broadcasted_iota(jnp.int32, (2 * slots, voc), 1) + me * voc

    def compute(index, plane):
        lhs = rows[pl.ds(pl.multiple_of(plane * 2 * slots, 2 * slots), 2 * slots), :]
        logits = jnp.dot(lhs, weight[...], preferred_element_type=jnp.float32)
        wanted = jnp.concatenate([
            jnp.sum(jnp.where(eye, tgt[plane * 2 + i][:, :slots], 0), axis=1, keepdims=True)
            for i in range(2)
        ], axis=0)
        top = jnp.max(logits, axis=1, keepdims=True)
        expo = jnp.exp(logits - top)
        parts = (
            top,
            jnp.sum(expo, axis=1, keepdims=True),
            jnp.sum(expo * logits, axis=1, keepdims=True),
            jnp.sum(jnp.where(voc_ids == wanted, logits, 0.0), axis=1, keepdims=True),
        )
        outbox[index] = jnp.concatenate(
            [jnp.sum(jnp.where(eye2, part, 0.0), axis=0, keepdims=True) for part in parts], axis=0)
        for k in range(8):
            if plane is z:
                if k == 0:
                    inbox[me] = outbox[index]
                    continue
                other = z * 8 + (me + k) % 8
            else:
                other = plane * 8 + (me + k) % 8
            pltpu.make_async_remote_copy(
                src_ref=outbox.at[index], dst_ref=inbox.at[me], send_sem=stat_send,
                recv_sem=stat_recv, device_id=(other // 4, other % 4), device_id_type=MESH,
            ).start()

    routes = {A1: [(B1, x_dev)], A2: [(B2, x_dev), (A2P, y_dev)], A3: [(B3, x_dev), (A3P, y_dev)], B1: [(B1P, y_dev)], B2: [(B2P, y_dev)], B3: [(B3P, y_dev)]}

    def take(*kinds):
        for kind in kinds:
            for sub in range(SUBS):
                piece = piece_of(block[kind], c, y if kind < XP else 1 - y, sub)
                arrived(piece, kind, sub)
                for later, device in routes.get(kind, ()):
                    push(piece, later, sub, device)
                push(piece, CORE + kind, sub, core_dev)

    def from_core(*kinds):
        for kind in kinds:
            for side, k in ((y, kind), (1 - y, OTHER_Y[kind])):
                for sub in range(SUBS):
                    arrived(piece_of(block[kind], 1 - c, side, sub), CORE + k, sub)

    take(A3)
    give(A1P)
    take(X, A2, A1)
    give(XP)
    take(B3, A3P, B2, A2P, B1)
    load.wait()
    for copy in tgt_copies:
        copy.wait()
    take(B3P)
    from_core(A3, B3)
    compute(0, z3)
    take(XP, A1P, B2P)
    from_core(A2, B2)
    compute(1, z2)
    take(B1P)
    from_core(X)
    compute(2, z)
    from_core(A1, B1)
    compute(3, z1)

    most = inbox.at[pl.ds(0, 31)]
    pltpu.make_async_copy(most, most, stat_recv).wait()
    every = inbox[...]
    tops = every[:, 0:1, :]
    top = jnp.max(tops, axis=0)
    share = jnp.exp(tops - top[None])
    total = jnp.sum(every[:, 1:2, :] * share, axis=0)
    weighted = jnp.sum(every[:, 2:3, :] * share, axis=0)
    picked = jnp.sum(every[:, 3:4, :], axis=0)
    lse = top + jnp.log(total)
    both = jnp.concatenate([picked - lse, lse - weighted / total], axis=0)
    result[...] = jnp.where(x == 0, both[:, :slots], both[:, slots:])

    for copy in started:
        copy.wait_send()
    pltpu.make_async_copy(most, most, stat_send).wait()


def fused_body(hidden, norm_gain, head_weight, targets, pad_mask):
    slots, depth = hidden.shape
    voc = head_weight.shape[1]
    vmem = pl.BlockSpec(memory_space=pltpu.VMEM)
    hbm = pl.BlockSpec(memory_space=pltpu.HBM)
    result = pl.pallas_call(
        kernel,
        out_shape=jax.ShapeDtypeStruct((2, slots), jnp.float32),
        in_specs=[hbm] * 4,
        out_specs=vmem,
        scratch_shapes=[
            pltpu.VMEM((slots, depth), jnp.bfloat16),
            pltpu.VMEM((1, depth), jnp.float32),
            pltpu.VMEM((1, slots), jnp.int32),
            pltpu.VMEM((8 * slots, depth), jnp.bfloat16),
            pltpu.VMEM((depth, voc), jnp.bfloat16),
            pltpu.VMEM((8, 1, 128), jnp.int32),
            pltpu.VMEM((4, 4, 128), jnp.float32),
            pltpu.VMEM((32, 4, 128), jnp.float32),
            pltpu.SemaphoreType.DMA((3,)),
            pltpu.SemaphoreType.DMA,
            pltpu.SemaphoreType.DMA((N_COPIES * SUBS,)),
            pltpu.SemaphoreType.DMA((N_COPIES * SUBS,)),
            pltpu.SemaphoreType.DMA((7,)),
            pltpu.SemaphoreType.DMA((7,)),
            pltpu.SemaphoreType.DMA,
            pltpu.SemaphoreType.DMA,
        ],
        compiler_params=pltpu.CompilerParams(
            collective_id=0, has_side_effects=True, vmem_limit_bytes=60 * 1024 * 1024),
    )(hidden, norm_gain.reshape(1, depth), head_weight, targets.reshape(1, slots))
    live = pad_mask.astype(jnp.float32)
    return (result[0] * live, result[1] * live)


def solution(mesh):
    fused = mesh.shape["req"] == 8 and mesh.shape["tp"] == 4
    return jax.shard_map(
        fused_body if fused else general_body,
        mesh=mesh,
        in_specs=(P("req", None), P(), P(None, ("req", "tp")), P("req"), P("req")),
        out_specs=(P("req"), P("req")),
        check_vma=False,
    )
```
